32 devices in a mesh: expert: 4 (over y, core), dp: 8 (over z, x).
Axes of the slice: x: 2, y: 2, z: 4, core: 2. Of those that a mesh axis runs over, the one named last changes fastest.
Arguments:
- tokens: bfloat16 [2048, 3584], P(('dp', 'expert')), parts along dimension 0, may hold values from -6 to 6
- expert_ids: int32 [2048, 1], P(('dp', 'expert')), parts along dimension 0, may hold values from 0 to 3; in each aligned block of 64 rows (0 to 63, 64 to 127, ...) at most 18 rows name the same one
- combine: bfloat16 [2048, 1], P(('dp', 'expert')), parts along dimension 0, may hold values from 0.19921875 to 1
- w_gate: bfloat16 [3584, 8192], P(None, 'expert'), may hold values from -0.09375 to 0.09375
- w_up: bfloat16 [3584, 8192], P(None, 'expert'), may hold values from -0.09375 to 0.09375
- w_down: bfloat16 [8192, 3584], P('expert'), may hold values from -0.125 to 0.125
Outputs:
- mixed: bfloat16 [2048, 3584], P(('dp', 'expert')), parts along dimension 0
The draws below stay inside these ranges and needn't reach their ends.
There are 8 independent parts, one for each index of `dp`. The reference program is written for one: setup_inputs(seed, part) draws one part's arguments, and reference() takes and returns one part's arrays. A program takes and returns all parts, laid end to end along the dimension named above; an argument that names none is the same for every part. Nothing has to cross between parts.
Inputs may be any that keep to these rules, and one draw needn't show every extreme that they name: `expert_ids`: each token names one expert. Among the 64 tokens of one device (aligned blocks of rows) no expert is named more than 18 times, a bound that some block reaches.
All inputs are finite; a program needn't handle non-finite values.
Results may differ from the reference program's by a relative error of at most 0.0057.
Values may be sent and summed in bfloat16 or wider, within the bound.
A program may use at most 128 MiB of HBM per device.

```python
import math
import jax
import jax.numpy as jnp
import numpy as np
from jax import lax

D = 3584
HW = 2048
EXPERTS = 4
TOP = 1
TOK_DEV = 64
CAP = 18
TOKENS = 256
SLICE = 2048
N_EXPERT = 4


def block_scale(stream_key, dims, cuts, smallest, top_value):
    loudness, own = 1.0, jax.random.fold_in(stream_key, 6)
    for axis_at, blocks in cuts:
        draws = jnp.exp(jax.random.uniform(jax.random.fold_in(own, axis_at), (blocks,), jnp.float32, smallest / len(cuts), top_value / len(cuts)))
        loudness = loudness * jnp.repeat(draws, dims[axis_at] // blocks).reshape([-1 if axis == axis_at else 1 for axis in range(len(dims))])
    return loudness


def routed_block(own_key, own, number, rows, number_of, top, most, skew):
    order = jax.random.permutation(own_key, number_of)
    heavy_load, common = shares(number_of, rows * top, most, skew, True), shares(number_of, rows * top, most, skew, False)
    places = jnp.arange(number_of)

    def named(tallies, offset_by):
        used = int((tallies > 0).sum())
        fixed = max(1, used // 4)
        shifted = fixed + (places - fixed + offset_by * (used - fixed)) % max(1, number_of - fixed)
        return jnp.zeros((number_of,), jnp.int32).at[order[jnp.where(places < fixed, places, shifted)]].set(jnp.asarray(tallies, jnp.int32))

    tallies = jnp.where(number % 4 == 0, named(heavy_load, number // 4), named(common, number - number // 4 - 1))
    mixed = jax.random.permutation(jax.random.fold_in(own, 3), number_of)
    source_of, sink = mixed[0:number_of // 2 * 2:2], mixed[1:number_of // 2 * 2:2]
    margin = jnp.minimum(tallies[source_of] - 1, most - tallies[sink]) // 2
    margin = jnp.where((source_of == order[0]) | (sink == order[0]) | (tallies[sink] == 0), 0, jnp.maximum(margin, 0))
    shifted = jax.random.randint(jax.random.fold_in(own, 4), (number_of // 2,), 0, 1 << 20) % (margin + 1)
    tallies = tallies.at[source_of].add(-shifted).at[sink].add(shifted)
    labels = jnp.searchsorted(jnp.cumsum(tallies), jnp.arange(rows * top), side="right").astype(jnp.int32)
    grid = labels.reshape(top, rows).T
    grid = grid[jax.random.permutation(jax.random.fold_in(own, 1), rows)]
    offset_by = jax.random.randint(jax.random.fold_in(own, 2), (rows, 1), 0, top)
    return jnp.take_along_axis(grid, (jnp.arange(top)[None, :] + offset_by) % top, axis=1)


def shares(amount, total, reach, skew, full):
    portions = [(1 << 20) // math.isqrt(rank ** skew) + 1 for rank in range(1, amount + 1)]
    largest = reach if full else min(reach, max(-(-total // amount), total * portions[0] // sum(portions)))
    least = 1 if total - largest >= amount - 1 else 0
    holding, surplus = [largest] + [least] * (amount - 1), total - largest - least * (amount - 1)
    while surplus > 0:
        free = [i for i in range(1, amount) if holding[i] < largest] or [i for i in range(1, amount) if holding[i] < reach]
        mass, remaining = sum([portions[i] for i in free]), surplus
        for i in free:
            addition = min(reach - holding[i], max(1, remaining * portions[i] // mass), surplus)
            holding[i] = holding[i] + addition
            surplus = surplus - addition
    return np.array(holding)


def scatter_about(own_key, shape, scale, reach, split=(), held_as=jnp.bfloat16):
    entries = jax.random.normal(own_key, shape, jnp.float32) * scale
    if len(split) > 0:
        entries = block_scale(own_key, shape, split, -0.22, 0.18) * entries
    return jnp.clip(entries, min=-reach, max=reach).astype(held_as)


def setup_inputs(seed: int = 0, part: int = 0) -> dict:
    streams_of = jax.random.split(jax.random.key(seed), 7)
    part_keys = jax.random.split(jax.random.fold_in(streams_of[6], part), 7)
    tokens = scatter_about(part_keys[0], (TOKENS, D), 1.0, 6.0, ((0, 4),))
    expert_ids_keys = jax.random.split(jax.random.fold_in(part_keys[1], 1), TOKENS // TOK_DEV)
    expert_ids_turns = jax.random.permutation(jax.random.fold_in(part_keys[1], 3), TOKENS // TOK_DEV)
    expert_ids = jax.vmap(lambda own, number: routed_block(jax.random.fold_in(part_keys[1], 2), own, number, TOK_DEV, EXPERTS, TOP, CAP, 2))(expert_ids_keys, expert_ids_turns).reshape((TOKENS, TOP))
    combine = jnp.clip(0.19921875 + 0.80078125 * jax.random.uniform(part_keys[2], (TOKENS, TOP), jnp.float32) ** block_scale(part_keys[2], (TOKENS, TOP), ((0, 4),), -0.2, 0.2), 0.19921875, 1.0).astype(jnp.bfloat16)
    w_gate = scatter_about(streams_of[3], (D, EXPERTS * HW), D ** -0.5, 0.09375, ((1, 4),))
    w_up = scatter_about(streams_of[4], (D, EXPERTS * HW), D ** -0.5, 0.09375, ((1, 4),))
    w_down = scatter_about(streams_of[5], (EXPERTS * HW, D), HW ** -0.5, 0.125, ((0, 4),))
    return {"tokens": tokens, "expert_ids": expert_ids, "combine": combine, "w_gate": w_gate, "w_up": w_up, "w_down": w_down}


def reference(tokens, expert_ids, combine, w_gate, w_up, w_down):
    accumulated = jnp.zeros((TOKENS, D), jnp.float32)
    weight_table = combine.astype(jnp.float32)
    span_size = N_EXPERT // EXPERTS
    for e in range(EXPERTS):
        gate_values = jnp.dot(tokens, w_gate[:, e * HW:(e + 1) * HW], preferred_element_type=jnp.float32)
        up_values = jnp.dot(tokens, w_up[:, e * HW:(e + 1) * HW], preferred_element_type=jnp.float32)
        hidden = (jax.nn.silu(gate_values) * up_values).astype(jnp.bfloat16)
        slice_total = jnp.zeros((TOKENS, D), jnp.float32)
        for s in range(span_size):
            first_row = e * HW + s * SLICE
            piece_out = jnp.dot(hidden[:, s * SLICE:(s + 1) * SLICE], w_down[first_row:first_row + SLICE, :], preferred_element_type=jnp.float32).astype(jnp.bfloat16)
            slice_total = slice_total + lax.optimization_barrier(piece_out).astype(jnp.float32)
        row_weight = jnp.sum(weight_table * (expert_ids == e).astype(jnp.float32), axis=1)
        accumulated = accumulated + row_weight[:, None] * slice_total
    return accumulated.astype(jnp.bfloat16)
```

```python
import functools

import jax
import jax.numpy as jnp
from jax import lax
from jax.experimental import pallas as pl
from jax.experimental.pallas import tpu as pltpu
from jax.sharding import PartitionSpec as P

EXPERTS = 4
TOP = 1
CAP = 18
MAIN = 16
EXTRA = CAP - MAIN
FOLD = 8
LANES = 128
PIECES = FOLD // EXTRA
CHUNK = PIECES * LANES
UNROLL = True
BF16, F32, I32 = jnp.bfloat16, jnp.float32, jnp.int32


def iota(shape, axis):
    return lax.broadcasted_iota(I32, shape, axis)


def dot(a, b):
    return jnp.dot(a, b, preferred_element_type=F32)


def extra_height(n):
    return -(-EXTRA * n // MAIN) * MAIN


def kernel(
    n, span, chunks, tokens_hbm, ids_hbm, combine_hbm, gate_hbm, up_hbm, down_hbm, out_hbm,
    tokens, ids, combine, gate, up, down, send_m, send_e, rows, recv_e, fold, gate_sum, up_sum,
    hidden, back_m, back_e, home, home_e, mixed,
    small_sem, late_sem, gate_sem, up_sem, down_sem, send_sem, recv_sem, back_sem, home_sem,
    send_e_sem, recv_e_sem, back_e_sem, home_e_sem, out_sem,
):
    me = lax.axis_index("expert")
    count = tokens.shape[0]
    width = gate.shape[2]
    mains = n * MAIN
    extras = n * EXTRA
    height = mains + extra_height(n)
    chip, core = me // 2, me % 2

    peers = []
    for step in range(1, n // 2):
        for turn in range(2):
            peers.append((chip + step) % (n // 2) * 2 + (core + turn) % 2)
    peers.append(chip * 2 + (core + 1) % 2)

    barrier = pltpu.get_barrier_semaphore()
    for peer in peers:
        pl.semaphore_signal(barrier, inc=1, device_id={"expert": peer})

    lead, rest = slice(0, CHUNK), slice(CHUNK, chunks * CHUNK)
    first = [
        pltpu.make_async_copy(ids_hbm, ids, small_sem.at[0]),
        pltpu.make_async_copy(tokens_hbm.at[:, lead], tokens.at[:, lead], small_sem.at[1]),
        pltpu.make_async_copy(tokens_hbm.at[:, rest], tokens.at[:, rest], small_sem.at[2]),
        pltpu.make_async_copy(combine_hbm, combine, small_sem.at[3]),
    ]
    for copy in first:
        copy.start()

    def gate_copy(k):
        part = pl.ds(pl.multiple_of(k * CHUNK, CHUNK), CHUNK)
        return pltpu.make_async_copy(gate_hbm.at[part, :], gate.at[k], gate_sem.at[k])

    def up_copy(k):
        part = pl.ds(pl.multiple_of(k * CHUNK, CHUNK), CHUNK)
        return pltpu.make_async_copy(up_hbm.at[part, :], up.at[k], up_sem.at[k])

    def down_copy(k):
        part = pl.ds(pl.multiple_of(k * CHUNK, CHUNK), CHUNK)
        return pltpu.make_async_copy(down_hbm.at[:, part], down.at[k], down_sem.at[k])

    last = chunks - 1
    tile = min(512, width)
    tiles = width // tile

    def late_copy(t, which):
        source, target = (gate_hbm, gate) if which == 0 else (up_hbm, up)
        lanes = slice(t * tile, (t + 1) * tile)
        return pltpu.make_async_copy(
            source.at[last * CHUNK:(last + 1) * CHUNK, lanes], target.at[last, :, lanes],
            late_sem.at[which, t],
        )

    def start_in(k, _):
        gate_copy(k).start()
        up_copy(k).start()
        return 0

    def start_down(k, _):
        down_copy(k).start()
        return 0

    lax.fori_loop(0, last, start_in, 0)
    for t in range(tiles):
        for which in range(2):
            late_copy(t, which).start()
    lax.fori_loop(0, chunks, start_down, 0)

    outs = slice(0, 1), slice(1, chunks)
    mid = (chunks + 1) // 2
    backs = slice(0, mid), slice(mid, chunks)

    def block_of(k):
        return pl.ds(pl.multiple_of(k * MAIN, MAIN), MAIN)

    def send_main(k, peer, source):
        return pltpu.make_async_remote_copy(
            src_ref=send_m.at[k, peer], dst_ref=rows.at[k, block_of(source), :],
            send_sem=send_sem.at[k, peer], recv_sem=recv_sem.at[k, source], device_id={"expert": peer},
        )

    def send_extra(half, peer, source):
        return pltpu.make_async_remote_copy(
            src_ref=send_e.at[peer, outs[half]], dst_ref=recv_e.at[source, outs[half]],
            send_sem=send_e_sem.at[half, peer], recv_sem=recv_e_sem.at[half, source],
            device_id={"expert": peer},
        )

    def back_main(k, peer, source):
        return pltpu.make_async_remote_copy(
            src_ref=back_m.at[k, peer], dst_ref=home.at[k, block_of(source), :],
            send_sem=back_sem.at[k, peer], recv_sem=home_sem.at[k, source], device_id={"expert": peer},
        )

    def back_extra(half, peer, source):
        return pltpu.make_async_remote_copy(
            src_ref=back_e.at[peer, backs[half]], dst_ref=home_e.at[source, backs[half]],
            send_sem=back_e_sem.at[half, peer], recv_sem=home_e_sem.at[half, source],
            device_id={"expert": peer},
        )

    def to_all(copy, at):
        for peer in peers:
            copy(at, peer, me).start()

    def from_all(copy, at):
        for peer in peers:
            copy(at, peer, peer).wait_recv()

    def sent_all(copy, at):
        for peer in peers:
            copy(at, peer, me).wait_send()

    row = iota((height, count), 0)
    tail = row - mains
    block = jnp.where(row < mains, row // MAIN, jnp.where(tail < extras, tail // EXTRA, -1))
    slot = jnp.where(row < mains, row % MAIN, MAIN + tail % EXTRA)
    earlier = (iota((count, count), 0) < iota((count, count), 1)).astype(F32).astype(BF16)

    first[0].wait()
    own = ids[...]
    member = iota((8, count), 0) == own
    ranks = dot(member.astype(F32).astype(BF16), earlier)
    place = jnp.sum(jnp.where(member, ranks, 0.0), axis=0, keepdims=True).astype(I32)
    low, high = own * span, own * span + span
    mask = (block >= low) & (block < high) & (slot == place)
    pick = jnp.where(mask, 1.0, 0.0).astype(BF16)

    def fold_extra(k, extra):
        for j in range(PIECES):
            fold[k, pl.ds(j, extras, stride=PIECES), :] = extra[:, j * LANES:(j + 1) * LANES]
        return fold[k].reshape(n, FOLD, LANES).astype(BF16)

    def push_main(k, block_m):
        send_m[k] = block_m.astype(BF16).reshape(n, MAIN, CHUNK)
        to_all(send_main, k)
        rows[k, block_of(me), :] = send_m[k, me]

    def push_extra(half):
        to_all(send_extra, half)
        recv_e[me, outs[half]] = send_e[me, outs[half]]

    first[1].wait()
    picked = dot(pick, tokens[:, lead])
    send_e[:, 0] = fold_extra(0, picked[mains:mains + extras])
    pl.semaphore_wait(barrier, n - 1)
    push_extra(0)
    push_main(0, picked[:mains])
    first[2].wait()
    picked = dot(pick[mains:], tokens[:, rest])
    for k in range(1, chunks):
        send_e[:, k] = fold_extra(k, picked[:extras, (k - 1) * CHUNK:k * CHUNK])
    push_extra(1)
    for k in range(1, chunks):
        push_main(k, dot(pick[:mains], tokens[:, k * CHUNK:(k + 1) * CHUNK]))

    first[3].wait()
    weight = combine[...].astype(F32)
    put = jnp.transpose(jnp.where(mask, weight, 0.0)).astype(BF16)

    def unfold(source, target, part):
        blank = jnp.zeros((height - mains - extras, CHUNK), F32)
        for k in range(part.start, part.stop):
            fold[k] = source[:, k].astype(F32).reshape(n * FOLD, LANES)
            parts = [fold[k, pl.ds(j, extras, stride=PIECES), :] for j in range(PIECES)]
            whole = jnp.concatenate(parts, axis=1)
            if height > mains + extras:
                whole = jnp.concatenate([whole, blank], axis=0)
            target[k, mains:, :] = whole.astype(BF16)

    def arrive(k):
        gate_copy(k).wait()
        up_copy(k).wait()
        from_all(send_main, k)

    from_all(send_extra, 0)
    unfold(recv_e, rows, outs[0])
    arrive(0)
    gate_sum[...] = dot(rows[0], gate[0])
    up_sum[...] = dot(rows[0], up[0])
    from_all(send_extra, 1)
    unfold(recv_e, rows, outs[1])

    def project(k, _):
        arrive(k)
        gate_sum[...] += dot(rows[k], gate[k])
        up_sum[...] += dot(rows[k], up[k])
        return 0

    if UNROLL:
        for k in range(1, last):
            project(k, 0)
    else:
        lax.fori_loop(1, last, project, 0)
    from_all(send_main, last)
    for t in range(tiles):
        part = slice(t * tile, (t + 1) * tile)
        late_copy(t, 0).wait()
        late_copy(t, 1).wait()
        g = gate_sum[:, part] + dot(rows[last], gate[last, :, part])
        u = up_sum[:, part] + dot(rows[last], up[last, :, part])
        hidden[:, part] = (g / (1.0 + jnp.exp(-g)) * u).astype(BF16)

    def finish(k):
        down_copy(k).wait()
        result = dot(hidden[...], down[k])
        back_m[k] = result[:mains].astype(BF16).reshape(n, MAIN, CHUNK)
        back_e[:, k] = fold_extra(k, result[mains:mains + extras])

    def give_back(k):
        to_all(back_main, k)
        home[k, block_of(me), :] = back_m[k, me]

    def give_extra(half):
        to_all(back_extra, half)
        home_e[me, backs[half]] = back_e[me, backs[half]]

    def step(k, _):
        finish(k)
        give_back(k)
        return 0

    lax.fori_loop(0, mid, step, 0)
    give_extra(0)
    lax.fori_loop(mid, last, step, 0)
    finish(last)
    give_extra(1)
    give_back(last)

    def out_copy(k):
        part = pl.ds(pl.multiple_of(k * CHUNK, CHUNK), CHUNK)
        return pltpu.make_async_copy(mixed.at[k], out_hbm.at[:, part], out_sem.at[k])

    def collect(k, _):
        from_all(back_main, k)
        out_hbm[:, pl.ds(pl.multiple_of(k * CHUNK, CHUNK), CHUNK)] = dot(put, home[k]).astype(BF16)
        return 0

    for half in range(2):
        from_all(back_extra, half)
        unfold(home_e, home, backs[half])
        lax.fori_loop(backs[half].start, backs[half].stop, collect, 0)

    def drain(k, _):
        sent_all(send_main, k)
        sent_all(back_main, k)
        return 0

    lax.fori_loop(0, chunks, drain, 0)
    for half in range(2):
        sent_all(send_extra, half)
        sent_all(back_extra, half)


def local(tokens, expert_ids, combine, w_gate, w_up, w_down):
    n = lax.axis_size("expert")
    span = n // EXPERTS
    count, model_width = tokens.shape
    width = w_gate.shape[1]
    chunks = model_width // CHUNK
    height = n * MAIN + extra_height(n)
    dma = pltpu.SemaphoreType.DMA
    vmem = pltpu.VMEM
    anywhere = pl.BlockSpec(memory_space=pltpu.HBM)
    packed = (n, chunks, FOLD, LANES)
    return pl.pallas_call(
        functools.partial(kernel, n, span, chunks),
        out_shape=pltpu.VMEM((count, model_width), BF16),
        in_specs=[anywhere] * 6,
        out_specs=pl.BlockSpec(memory_space=pltpu.VMEM),
        scratch_shapes=[
            vmem((count, model_width), BF16),
            vmem((1, count), I32),
            vmem((1, count), BF16),
            vmem((chunks, CHUNK, width), BF16),
            vmem((chunks, CHUNK, width), BF16),
            vmem((chunks, width, CHUNK), BF16),
            vmem((chunks, n, MAIN, CHUNK), BF16),
            vmem(packed, BF16),
            vmem((chunks, height, CHUNK), BF16),
            vmem(packed, BF16),
            vmem((chunks, n * FOLD, LANES), F32),
            vmem((height, width), F32),
            vmem((height, width), F32),
            vmem((height, width), BF16),
            vmem((chunks, n, MAIN, CHUNK), BF16),
            vmem(packed, BF16),
            vmem((chunks, height, CHUNK), BF16),
            vmem(packed, BF16),
            vmem((chunks, count, CHUNK), BF16),
            dma((4,)),
            dma((2, max(1, width // 512))),
            dma((chunks,)),
            dma((chunks,)),
            dma((chunks,)),
            dma((chunks, n)),
            dma((chunks, n)),
            dma((chunks, n)),
            dma((chunks, n)),
            dma((2, n)),
            dma((2, n)),
            dma((2, n)),
            dma((2, n)),
            dma((chunks,)),
        ],
        compiler_params=pltpu.CompilerParams(
            collective_id=0, vmem_limit_bytes=54 * 1024 * 1024
        ),
    )(
        tokens,
        expert_ids.reshape(1, count),
        combine.reshape(1, count),
        w_gate,
        w_up,
        w_down,
    )


def solution(mesh):
    placed = (
        P(("dp", "expert"), None),
        P(("dp", "expert"), None),
        P(("dp", "expert"), None),
        P(None, "expert"),
        P(None, "expert"),
        P("expert", None),
    )
    return jax.shard_map(
        local, mesh=mesh, in_specs=placed, out_specs=P(("dp", "expert"), None), check_vma=False
    )
```

```python
import functools

import jax
import jax.numpy as jnp
from jax import lax
from jax.experimental import pallas as pl
from jax.experimental.pallas import tpu as pltpu
from jax.sharding import PartitionSpec as P

EXPERTS = 4
TOP = 1
CAP = 18
MAIN = 16
EXTRA = CAP - MAIN
FOLD = 8
LANES = 128
PIECES = FOLD // EXTRA
CHUNK = PIECES * LANES
SPAN_ROWS = 128
EARLY, DOWN_AT, DOWN_N = 6, 2, 2
BF16, F32, I32 = jnp.bfloat16, jnp.float32, jnp.int32


def iota(shape, axis):
    return lax.broadcasted_iota(I32, shape, axis)


def dot(a, b):
    return jnp.dot(a, b, preferred_element_type=F32)


def padded(height):
    return -(-height // SPAN_ROWS) * SPAN_ROWS


def extra_height(n):
    return -(-EXTRA * n // MAIN) * MAIN


def kernel(
    n, span, chunks, tokens_hbm, ids_hbm, combine_hbm, gate_hbm, up_hbm, down_hbm, out_vmem,
    tokens, ids, combine, gate, up, down, send_m, send_e, rows, recv_e, fold, gate_sum, up_sum,
    hidden, back_m, back_e, home, home_e,
    small_sem, late_sem, gate_sem, up_sem, down_sem, send_sem, recv_sem, back_sem, home_sem,
    send_e_sem, recv_e_sem, back_e_sem, home_e_sem,
):
    me = lax.axis_index("expert")
    count = tokens.shape[0]
    width = gate.shape[2]
    mains = n * MAIN
    extras = n * EXTRA
    height = mains + extra_height(n)
    chip, core = me // 2, me % 2

    peers = []
    for step in range(1, n // 2):
        for turn in range(2):
            peers.append((chip + step) % (n // 2) * 2 + (core + turn) % 2)
    peers.append(chip * 2 + (core + 1) % 2)

    barrier = pltpu.get_barrier_semaphore()
    lead, rest = slice(0, CHUNK), slice(CHUNK, chunks * CHUNK)
    first = [
        pltpu.make_async_copy(ids_hbm, ids, small_sem.at[0]),
        pltpu.make_async_copy(tokens_hbm.at[:, lead], tokens.at[:, lead], small_sem.at[1]),
        pltpu.make_async_copy(tokens_hbm.at[:, rest], tokens.at[:, rest], small_sem.at[2]),
        pltpu.make_async_copy(combine_hbm, combine, small_sem.at[3]),
    ]
    for copy in first:
        copy.start()

    def gate_copy(k):
        part = pl.ds(pl.multiple_of(k * CHUNK, CHUNK), CHUNK)
        return pltpu.make_async_copy(gate_hbm.at[part, :], gate.at[k], gate_sem.at[k])

    def up_copy(k):
        part = pl.ds(pl.multiple_of(k * CHUNK, CHUNK), CHUNK)
        return pltpu.make_async_copy(up_hbm.at[part, :], up.at[k], up_sem.at[k])

    def down_copy(k):
        part = pl.ds(pl.multiple_of(k * CHUNK, CHUNK), CHUNK)
        return pltpu.make_async_copy(down_hbm.at[:, part], down.at[k], down_sem.at[k])

    last = chunks - 1
    tile = min(512, width)
    tiles = width // tile

    def late_copy(t, which):
        source, target = (gate_hbm, gate) if which == 0 else (up_hbm, up)
        lanes = slice(t * tile, (t + 1) * tile)
        return pltpu.make_async_copy(
            source.at[last * CHUNK:(last + 1) * CHUNK, lanes], target.at[last, :, lanes],
            late_sem.at[which, t],
        )

    def start_in(k, _):
        gate_copy(k).start()
        up_copy(k).start()
        return 0

    def start_down(k, _):
        down_copy(k).start()
        return 0

    start_in(0, 0)
    for peer in peers:
        pl.semaphore_signal(barrier, inc=1, device_id={"expert": peer})
    early = min(EARLY, last)
    lax.fori_loop(1, early, start_in, 0)

    outs = slice(0, 1), slice(1, chunks)
    mid = (chunks + 1) // 2
    backs = slice(0, mid), slice(mid, chunks)

    def block_of(k):
        return pl.ds(pl.multiple_of(k * MAIN, MAIN), MAIN)

    def send_main(k, peer, source):
        return pltpu.make_async_remote_copy(
            src_ref=send_m.at[k, peer], dst_ref=rows.at[k, block_of(source), :],
            send_sem=send_sem.at[k, peer], recv_sem=recv_sem.at[k, source], device_id={"expert": peer},
        )

    def send_extra(half, peer, source):
        return pltpu.make_async_remote_copy(
            src_ref=send_e.at[peer, outs[half]], dst_ref=recv_e.at[source, outs[half]],
            send_sem=send_e_sem.at[half, peer], recv_sem=recv_e_sem.at[half, source],
            device_id={"expert": peer},
        )

    def back_main(k, peer, source):
        return pltpu.make_async_remote_copy(
            src_ref=back_m.at[k, peer], dst_ref=home.at[k, block_of(source), :],
            send_sem=back_sem.at[k, peer], recv_sem=home_sem.at[k, source], device_id={"expert": peer},
        )

    def back_extra(half, peer, source):
        return pltpu.make_async_remote_copy(
            src_ref=back_e.at[peer, backs[half]], dst_ref=home_e.at[source, backs[half]],
            send_sem=back_e_sem.at[half, peer], recv_sem=home_e_sem.at[half, source],
            device_id={"expert": peer},
        )

    def to_all(copy, at):
        for peer in peers:
            copy(at, peer, me).start()

    def from_all(copy, at):
        for peer in peers:
            copy(at, peer, peer).wait_recv()

    def sent_all(copy, at):
        for peer in peers:
            copy(at, peer, me).wait_send()

    row = iota((height, count), 0)
    tail = row - mains
    block = jnp.where(row < mains, row // MAIN, jnp.where(tail < extras, tail // EXTRA, -1))
    slot = jnp.where(row < mains, row % MAIN, MAIN + tail % EXTRA)
    earlier = (iota((count, count), 0) < iota((count, count), 1)).astype(F32).astype(BF16)

    full = rows.shape[1]
    rows[:, height:, :] = jnp.zeros((chunks, full - height, CHUNK), BF16)
    hidden[height:, :] = jnp.zeros((full - height, width), BF16)

    first[0].wait()
    own = ids[...]
    member = iota((8, count), 0) == own
    ranks = dot(member.astype(F32).astype(BF16), earlier)
    place = jnp.sum(jnp.where(member, ranks, 0.0), axis=0, keepdims=True).astype(I32)
    low, high = own * span, own * span + span
    mask = (block >= low) & (block < high) & (slot == place)
    pick = jnp.where(mask, 1.0, 0.0).astype(BF16)

    def fold_extra(k, extra):
        for j in range(PIECES):
            fold[k, pl.ds(j, extras, stride=PIECES), :] = extra[:, j * LANES:(j + 1) * LANES]
        return fold[k].reshape(n, FOLD, LANES).astype(BF16)

    def push_main(k, block_m):
        send_m[k] = block_m.astype(BF16).reshape(n, MAIN, CHUNK)
        to_all(send_main, k)
        rows[k, block_of(me), :] = send_m[k, me]

    def push_extra(half):
        to_all(send_extra, half)
        recv_e[me, outs[half]] = send_e[me, outs[half]]

    first[1].wait()
    picked = dot(pick, tokens[:, lead])
    send_e[:, 0] = fold_extra(0, picked[mains:mains + extras])
    pl.semaphore_wait(barrier, n - 1)
    push_extra(0)
    push_main(0, picked[:mains])
    first[2].wait()
    picked = dot(pick[mains:], tokens[:, rest])
    for k in range(1, chunks):
        send_e[:, k] = fold_extra(k, picked[:extras, (k - 1) * CHUNK:k * CHUNK])
    push_extra(1)
    for k in range(1, chunks):
        push_main(k, dot(pick[:mains], tokens[:, k * CHUNK:(k + 1) * CHUNK]))

    first[3].wait()
    weight = combine[...].astype(F32)
    put = jnp.transpose(jnp.where(mask, weight, 0.0)).astype(BF16)

    def unfold(source, target, part):
        blank = jnp.zeros((height - mains - extras, CHUNK), F32)
        for k in range(part.start, part.stop):
            fold[k] = source[:, k].astype(F32).reshape(n * FOLD, LANES)
            parts = [fold[k, pl.ds(j, extras, stride=PIECES), :] for j in range(PIECES)]
            whole = jnp.concatenate(parts, axis=1)
            if height > mains + extras:
                whole = jnp.concatenate([whole, blank], axis=0)
            target[k, mains:height, :] = whole.astype(BF16)

    def arrive(k):
        gate_copy(k).wait()
        up_copy(k).wait()
        from_all(send_main, k)

    lax.fori_loop(early, last, start_in, 0)
    for t in range(tiles):
        for which in range(2):
            late_copy(t, which).start()

    from_all(send_extra, 0)
    unfold(recv_e, rows, outs[0])
    arrive(0)
    gate_sum[...] = dot(rows[0], gate[0])
    up_sum[...] = dot(rows[0], up[0])
    from_all(send_extra, 1)
    unfold(recv_e, rows, outs[1])

    def project(k, _):
        arrive(k)
        gate_sum[...] += dot(rows[k], gate[k])
        up_sum[...] += dot(rows[k], up[k])
        return 0

    for k in range(1, last):
        project(k, 0)
        if k == DOWN_AT:
            lax.fori_loop(0, DOWN_N, start_down, 0)
        if k == last - 1:
            lax.fori_loop(DOWN_N, chunks, start_down, 0)
    from_all(send_main, last)

    def activate(t):
        part = slice(t * tile, (t + 1) * tile)
        g = gate_sum[:height, part]
        hidden[:height, part] = (g / (1.0 + jnp.exp(-g)) * up_sum[:height, part]).astype(BF16)

    for t in range(tiles):
        part = slice(t * tile, (t + 1) * tile)
        late_copy(t, 0).wait()
        late_copy(t, 1).wait()
        gate_sum[:, part] += dot(rows[last], gate[last, :, part])
        up_sum[:, part] += dot(rows[last], up[last, :, part])
        if t > 0:
            activate(t - 1)
    activate(tiles - 1)

    def finish(k):
        down_copy(k).wait()
        result = dot(hidden[...], down[k])
        back_m[k] = result[:mains].astype(BF16).reshape(n, MAIN, CHUNK)
        back_e[:, k] = fold_extra(k, result[mains:mains + extras])

    def give_back(k):
        to_all(back_main, k)
        home[k, block_of(me), :] = back_m[k, me]

    def give_extra(half):
        to_all(back_extra, half)
        home_e[me, backs[half]] = back_e[me, backs[half]]

    def step(k, _):
        finish(k)
        give_back(k)
        return 0

    lax.fori_loop(0, mid, step, 0)
    give_extra(0)
    lax.fori_loop(mid, last, step, 0)
    finish(last)
    give_extra(1)
    give_back(last)

    def combine_chunk(k):
        from_all(back_main, k)
        part = pl.ds(pl.multiple_of(k * CHUNK, CHUNK), CHUNK)
        out_vmem[:, part] = dot(put, home[k]).astype(BF16)

    def collect(k, _):
        combine_chunk(k)
        sent_all(back_main, k)
        return 0

    def drain(k, _):
        sent_all(send_main, k)
        return 0

    lax.fori_loop(0, chunks, drain, 0)
    sent_all(send_extra, 0)
    sent_all(send_extra, 1)
    for half in range(2):
        from_all(back_extra, half)
        unfold(home_e, home, backs[half])
        sent_all(back_extra, half)
        lax.fori_loop(backs[half].start, min(backs[half].stop, last), collect, 0)
    combine_chunk(last)
    sent_all(back_main, last)


def local(tokens, expert_ids, combine, w_gate, w_up, w_down):
    n = lax.axis_size("expert")
    span = n // EXPERTS
    count, model_width = tokens.shape
    width = w_gate.shape[1]
    chunks = model_width // CHUNK
    height = n * MAIN + extra_height(n)
    dma = pltpu.SemaphoreType.DMA
    vmem = pltpu.VMEM
    anywhere = pl.BlockSpec(memory_space=pltpu.HBM)
    packed = (n, chunks, FOLD, LANES)
    return pl.pallas_call(
        functools.partial(kernel, n, span, chunks),
        out_shape=pltpu.VMEM((count, model_width), BF16),
        in_specs=[anywhere] * 6,
        out_specs=pl.BlockSpec(memory_space=pltpu.VMEM),
        scratch_shapes=[
            vmem((count, model_width), BF16),
            vmem((1, count), I32),
            vmem((1, count), BF16),
            vmem((chunks, CHUNK, width), BF16),
            vmem((chunks, CHUNK, width), BF16),
            vmem((chunks, width, CHUNK), BF16),
            vmem((chunks, n, MAIN, CHUNK), BF16),
            vmem(packed, BF16),
            vmem((chunks, padded(height), CHUNK), BF16),
            vmem(packed, BF16),
            vmem((chunks, n * FOLD, LANES), F32),
            vmem((padded(height), width), F32),
            vmem((padded(height), width), F32),
            vmem((padded(height), width), BF16),
            vmem((chunks, n, MAIN, CHUNK), BF16),
            vmem(packed, BF16),
            vmem((chunks, height, CHUNK), BF16),
            vmem(packed, BF16),
            dma((4,)),
            dma((2, max(1, width // 512))),
            dma((chunks,)),
            dma((chunks,)),
            dma((chunks,)),
            dma((chunks, n)),
            dma((chunks, n)),
            dma((chunks, n)),
            dma((chunks, n)),
            dma((2, n)),
            dma((2, n)),
            dma((2, n)),
            dma((2, n)),
        ],
        compiler_params=pltpu.CompilerParams(
            collective_id=0, vmem_limit_bytes=54 * 1024 * 1024
        ),
    )(
        tokens,
        expert_ids.reshape(1, count),
        combine.reshape(1, count),
        w_gate,
        w_up,
        w_down,
    )


def solution(mesh):
    placed = (
        P(("dp", "expert"), None),
        P(("dp", "expert"), None),
        P(("dp", "expert"), None),
        P(None, "expert"),
        P(None, "expert"),
        P("expert", None),
    )
    return jax.shard_map(
        local, mesh=mesh, in_specs=placed, out_specs=P(("dp", "expert"), None), check_vma=False
    )
```

```python
import functools

import jax
import jax.numpy as jnp
from jax import lax
from jax.experimental import pallas as pl
from jax.experimental.pallas import tpu as pltpu
from jax.sharding import PartitionSpec as P

EXPERTS = 4
TOP = 1
CAP = 18
MAIN = 16
EXTRA = CAP - MAIN
FOLD = 8
LANES = 128
PIECES = FOLD // EXTRA
CHUNK = PIECES * LANES
SPAN_ROWS = 128
EARLY, DOWN_AT, DOWN_N = 6, 2, 2
BF16, F32, I32 = jnp.bfloat16, jnp.float32, jnp.int32


def iota(shape, axis):
    return lax.broadcasted_iota(I32, shape, axis)


def dot(a, b):
    return jnp.dot(a, b, preferred_element_type=F32)


def padded(height):
    return -(-height // SPAN_ROWS) * SPAN_ROWS


def extra_height(n):
    return -(-EXTRA * n // MAIN) * MAIN


def kernel(
    n, span, chunks, tokens_hbm, ids_hbm, combine_hbm, gate_hbm, up_hbm, down_hbm, out_vmem,
    tokens, ids, combine, gate, up, down, send_m, send_e, rows, recv_e, fold, gate_sum, up_sum,
    hidden, back_m, back_e, home, home_e,
    small_sem, late_sem, gate_sem, up_sem, down_sem, send_sem, recv_sem, back_sem, home_sem,
    send_e_sem, recv_e_sem, back_e_sem, home_e_sem,
):
    me = lax.axis_index("expert")
    count = tokens.shape[0]
    width = gate.shape[2]
    mains = n * MAIN
    extras = n * EXTRA
    height = mains + extra_height(n)
    chip, core = me // 2, me % 2

    peers = []
    for step in range(1, n // 2):
        for turn in range(2):
            peers.append((chip + step) % (n // 2) * 2 + (core + turn) % 2)
    peers.append(chip * 2 + (core + 1) % 2)

    barrier = pltpu.get_barrier_semaphore()
    lead, rest = slice(0, CHUNK), slice(CHUNK, chunks * CHUNK)
    first = [
        pltpu.make_async_copy(ids_hbm, ids, small_sem.at[0]),
        pltpu.make_async_copy(tokens_hbm.at[:, lead], tokens.at[:, lead], small_sem.at[1]),
        pltpu.make_async_copy(tokens_hbm.at[:, rest], tokens.at[:, rest], small_sem.at[2]),
        pltpu.make_async_copy(combine_hbm, combine, small_sem.at[3]),
    ]
    for copy in first:
        copy.start()

    def gate_copy(k):
        part = pl.ds(pl.multiple_of(k * CHUNK, CHUNK), CHUNK)
        return pltpu.make_async_copy(gate_hbm.at[part, :], gate.at[k], gate_sem.at[k])

    def up_copy(k):
        part = pl.ds(pl.multiple_of(k * CHUNK, CHUNK), CHUNK)
        return pltpu.make_async_copy(up_hbm.at[part, :], up.at[k], up_sem.at[k])

    def down_copy(k):
        part = pl.ds(pl.multiple_of(k * CHUNK, CHUNK), CHUNK)
        return pltpu.make_async_copy(down_hbm.at[:, part], down.at[k], down_sem.at[k])

    last = chunks - 1
    tile = min(512, width)
    tiles = width // tile

    def late_copy(t, which):
        source, target = (gate_hbm, gate) if which == 0 else (up_hbm, up)
        lanes = slice(t * tile, (t + 1) * tile)
        return pltpu.make_async_copy(
            source.at[last * CHUNK:(last + 1) * CHUNK, lanes], target.at[last, :, lanes],
            late_sem.at[which, t],
        )

    def start_in(k, _):
        gate_copy(k).start()
        up_copy(k).start()
        return 0

    def start_down(k, _):
        down_copy(k).start()
        return 0

    start_in(0, 0)
    for peer in peers:
        pl.semaphore_signal(barrier, inc=1, device_id={"expert": peer})
    early = min(EARLY, last)
    lax.fori_loop(1, early, start_in, 0)

    outs = slice(0, 1), slice(1, chunks)
    mid = (chunks + 1) // 2
    backs = slice(0, mid), slice(mid, chunks)

    def block_of(k):
        return pl.ds(pl.multiple_of(k * MAIN, MAIN), MAIN)

    def send_main(k, peer, source):
        return pltpu.make_async_remote_copy(
            src_ref=send_m.at[k, peer], dst_ref=rows.at[k, block_of(source), :],
            send_sem=send_sem.at[k, peer], recv_sem=recv_sem.at[k, source], device_id={"expert": peer},
        )

    def send_extra(half, peer, source):
        return pltpu.make_async_remote_copy(
            src_ref=send_e.at[peer, outs[half]], dst_ref=recv_e.at[source, outs[half]],
            send_sem=send_e_sem.at[half, peer], recv_sem=recv_e_sem.at[half, source],
            device_id={"expert": peer},
        )

    def back_main(k, peer, source):
        return pltpu.make_async_remote_copy(
            src_ref=back_m.at[k, peer], dst_ref=home.at[k, block_of(source), :],
            send_sem=back_sem.at[k, peer], recv_sem=home_sem.at[k, source], device_id={"expert": peer},
        )

    def back_extra(half, peer, source):
        return pltpu.make_async_remote_copy(
            src_ref=back_e.at[peer, backs[half]], dst_ref=home_e.at[source, backs[half]],
            send_sem=back_e_sem.at[half, peer], recv_sem=home_e_sem.at[half, source],
            device_id={"expert": peer},
        )

    def to_all(copy, at):
        for peer in peers:
            copy(at, peer, me).start()

    def from_all(copy, at):
        for peer in peers:
            copy(at, peer, peer).wait_recv()

    def sent_all(copy, at):
        for peer in peers:
            copy(at, peer, me).wait_send()

    row = iota((height, count), 0)
    tail = row - mains
    block = jnp.where(row < mains, row // MAIN, jnp.where(tail < extras, tail // EXTRA, -1))
    slot = jnp.where(row < mains, row % MAIN, MAIN + tail % EXTRA)
    earlier = (iota((count, count), 0) < iota((count, count), 1)).astype(F32).astype(BF16)

    full = rows.shape[1]
    rows[:, height:, :] = jnp.zeros((chunks, full - height, CHUNK), BF16)
    hidden[height:, :] = jnp.zeros((full - height, width), BF16)

    first[0].wait()
    own = ids[...]
    member = iota((8, count), 0) == own
    ranks = dot(member.astype(F32).astype(BF16), earlier)
    place = jnp.sum(jnp.where(member, ranks, 0.0), axis=0, keepdims=True).astype(I32)
    low, high = own * span, own * span + span
    mask = (block >= low) & (block < high) & (slot == place)
    pick = jnp.where(mask, 1.0, 0.0).astype(BF16)

    def fold_extra(k, extra):
        for j in range(PIECES):
            fold[k, pl.ds(j, extras, stride=PIECES), :] = extra[:, j * LANES:(j + 1) * LANES]
        return fold[k, :n * FOLD].reshape(n, FOLD, LANES).astype(BF16)

    def push_main(k, block_m):
        send_m[k] = block_m.astype(BF16).reshape(n, MAIN, CHUNK)
        to_all(send_main, k)
        rows[k, block_of(me), :] = send_m[k, me]

    def push_extra(half):
        to_all(send_extra, half)
        recv_e[me, outs[half]] = send_e[me, outs[half]]

    first[1].wait()
    picked = dot(pick, tokens[:, lead])
    send_e[:, 0] = fold_extra(0, picked[mains:mains + extras])
    pl.semaphore_wait(barrier, n - 1)
    push_extra(0)
    push_main(0, picked[:mains])
    first[2].wait()
    picked = dot(pick[mains:], tokens[:, rest])
    for k in range(1, chunks):
        send_e[:, k] = fold_extra(k, picked[:extras, (k - 1) * CHUNK:k * CHUNK])
    push_extra(1)
    for k in range(1, chunks):
        push_main(k, dot(pick[:mains], tokens[:, k * CHUNK:(k + 1) * CHUNK]))

    first[3].wait()
    weight = combine[...].astype(F32)
    put = jnp.transpose(jnp.where(mask, weight, 0.0)).astype(BF16)

    def unfold(source, target, part):
        blank = jnp.zeros((height - mains - extras, CHUNK), F32)
        for k in range(part.start, part.stop):
            fold[k, :n * FOLD] = source[:, k].astype(F32).reshape(n * FOLD, LANES)
            parts = [fold[k, pl.ds(j, extras, stride=PIECES), :] for j in range(PIECES)]
            whole = jnp.concatenate(parts, axis=1)
            if height > mains + extras:
                whole = jnp.concatenate([whole, blank], axis=0)
            target[k, mains:height, :] = whole.astype(BF16)

    def arrive(k):
        gate_copy(k).wait()
        up_copy(k).wait()
        from_all(send_main, k)

    lax.fori_loop(early, last, start_in, 0)
    for t in range(tiles):
        for which in range(2):
            late_copy(t, which).start()

    from_all(send_extra, 0)
    unfold(recv_e, rows, outs[0])
    arrive(0)
    gate_sum[...] = dot(rows[0], gate[0])
    up_sum[...] = dot(rows[0], up[0])
    from_all(send_extra, 1)
    unfold(recv_e, rows, outs[1])

    def project(k, _):
        arrive(k)
        gate_sum[...] += dot(rows[k], gate[k])
        up_sum[...] += dot(rows[k], up[k])
        return 0

    for k in range(1, last):
        project(k, 0)
        if k == DOWN_AT:
            lax.fori_loop(0, DOWN_N, start_down, 0)
        if k == last - 1:
            lax.fori_loop(DOWN_N, chunks, start_down, 0)
    from_all(send_main, last)

    def activate(t):
        part = slice(t * tile, (t + 1) * tile)
        g = gate_sum[:height, part]
        hidden[:height, part] = (g / (1.0 + jnp.exp(-g)) * up_sum[:height, part]).astype(BF16)

    for t in range(tiles):
        part = slice(t * tile, (t + 1) * tile)
        late_copy(t, 0).wait()
        late_copy(t, 1).wait()
        gate_sum[:, part] += dot(rows[last], gate[last, :, part])
        up_sum[:, part] += dot(rows[last], up[last, :, part])
        if t > 0:
            activate(t - 1)
    activate(tiles - 1)

    def finish(k):
        down_copy(k).wait()
        result = dot(hidden[...], down[k])
        back_m[k] = result[:mains].astype(BF16).reshape(n, MAIN, CHUNK)
        back_e[:, k] = fold_extra(k, result[mains:mains + extras])

    def give_back(k):
        to_all(back_main, k)
        home[k, block_of(me), :] = back_m[k, me]

    def give_extra(half):
        to_all(back_extra, half)
        home_e[me, backs[half]] = back_e[me, backs[half]]

    def step(k, _):
        finish(k)
        give_back(k)
        return 0

    lax.fori_loop(0, mid, step, 0)
    give_extra(0)
    lax.fori_loop(mid, last, step, 0)
    finish(last)
    give_extra(1)
    give_back(last)

    def combine_chunk(k):
        from_all(back_main, k)
        part = pl.ds(pl.multiple_of(k * CHUNK, CHUNK), CHUNK)
        out_vmem[:, part] = dot(put, home[k]).astype(BF16)

    def collect(k, _):
        combine_chunk(k)
        sent_all(back_main, k)
        return 0

    def drain(k, _):
        sent_all(send_main, k)
        return 0

    lax.fori_loop(0, chunks, drain, 0)
    sent_all(send_extra, 0)
    sent_all(send_extra, 1)
    for half in range(2):
        from_all(back_extra, half)
        unfold(home_e, home, backs[half])
        sent_all(back_extra, half)
        lax.fori_loop(backs[half].start, min(backs[half].stop, last), collect, 0)
    combine_chunk(last)
    sent_all(back_main, last)


def local(tokens, expert_ids, combine, w_gate, w_up, w_down):
    n = lax.axis_size("expert")
    span = n // EXPERTS
    count, model_width = tokens.shape
    width = w_gate.shape[1]
    chunks = model_width // CHUNK
    height = n * MAIN + extra_height(n)
    dma = pltpu.SemaphoreType.DMA
    vmem = pltpu.VMEM
    anywhere = pl.BlockSpec(memory_space=pltpu.HBM)
    packed = (n, chunks, FOLD, LANES)
    return pl.pallas_call(
        functools.partial(kernel, n, span, chunks),
        out_shape=pltpu.VMEM((count, model_width), BF16),
        in_specs=[anywhere] * 6,
        out_specs=pl.BlockSpec(memory_space=pltpu.VMEM),
        scratch_shapes=[
            vmem((count, model_width), BF16),
            vmem((1, count), I32),
            vmem((1, count), BF16),
            vmem((chunks, CHUNK, width), BF16),
            vmem((chunks, CHUNK, width), BF16),
            vmem((chunks, width, CHUNK), BF16),
            vmem((chunks, n, MAIN, CHUNK), BF16),
            vmem(packed, BF16),
            vmem((chunks, padded(height), CHUNK), BF16),
            vmem(packed, BF16),
            vmem((chunks, (n + 1) * FOLD, LANES), F32),
            vmem((padded(height), width), F32),
            vmem((padded(height), width), F32),
            vmem((padded(height), width), BF16),
            vmem((chunks, n, MAIN, CHUNK), BF16),
            vmem(packed, BF16),
            vmem((chunks, height, CHUNK), BF16),
            vmem(packed, BF16),
            dma((4,)),
            dma((2, max(1, width // 512))),
            dma((chunks,)),
            dma((chunks,)),
            dma((chunks,)),
            dma((chunks, n)),
            dma((chunks, n)),
            dma((chunks, n)),
            dma((chunks, n)),
            dma((2, n)),
            dma((2, n)),
            dma((2, n)),
            dma((2, n)),
        ],
        compiler_params=pltpu.CompilerParams(
            collective_id=0, vmem_limit_bytes=54 * 1024 * 1024
        ),
    )(
        tokens,
        expert_ids.reshape(1, count),
        combine.reshape(1, count),
        w_gate,
        w_up,
        w_down,
    )


def solution(mesh):
    placed = (
        P(("dp", "expert"), None),
        P(("dp", "expert"), None),
        P(("dp", "expert"), None),
        P(None, "expert"),
        P(None, "expert"),
        P("expert", None),
    )
    return jax.shard_map(
        local, mesh=mesh, in_specs=placed, out_specs=P(("dp", "expert"), None), check_vma=False
    )
```

```python
import functools

import jax
import jax.numpy as jnp
from jax import lax
from jax.experimental import pallas as pl
from jax.experimental.pallas import tpu as pltpu
from jax.sharding import PartitionSpec as P

EXPERTS = 4
TOP = 1
CAP = 18
MAIN = 16
EXTRA = CAP - MAIN
FOLD = 8
LANES = 128
PIECES = FOLD // EXTRA
CHUNK = PIECES * LANES
SPAN_ROWS = 128
EARLY, DOWN_AT, DOWN_N = 6, 2, 2
BF16, F32, I32 = jnp.bfloat16, jnp.float32, jnp.int32


def iota(shape, axis):
    return lax.broadcasted_iota(I32, shape, axis)


def dot(a, b):
    return jnp.dot(a, b, preferred_element_type=F32)


def padded(height):
    return -(-height // SPAN_ROWS) * SPAN_ROWS


def extra_height(n):
    return -(-EXTRA * n // MAIN) * MAIN


def kernel(
    n, span, chunks, tokens_hbm, ids_hbm, combine_hbm, gate_hbm, up_hbm, down_hbm, out_vmem,
    tokens, ids, combine, gate, up, down, send_m, send_e, rows, recv_e, fold, gate_sum, up_sum,
    hidden, back_m, back_e, home, home_e,
    small_sem, late_sem, gate_sem, up_sem, down_sem, send_sem, recv_sem, back_sem, home_sem,
    send_e_sem, recv_e_sem, back_e_sem, home_e_sem,
):
    me = lax.axis_index("expert")
    count = tokens.shape[0]
    width = gate.shape[2]
    mains = n * MAIN
    extras = n * EXTRA
    height = mains + extra_height(n)
    chip, core = me // 2, me % 2

    peers = []
    for step in range(1, n // 2):
        for turn in range(2):
            peers.append((chip + step) % (n // 2) * 2 + (core + turn) % 2)
    peers.append(chip * 2 + (core + 1) % 2)

    barrier = pltpu.get_barrier_semaphore()
    lead, rest = slice(0, CHUNK), slice(CHUNK, chunks * CHUNK)
    first = [
        pltpu.make_async_copy(ids_hbm, ids, small_sem.at[0]),
        pltpu.make_async_copy(tokens_hbm.at[:, lead], tokens.at[:, lead], small_sem.at[1]),
        pltpu.make_async_copy(tokens_hbm.at[:, rest], tokens.at[:, rest], small_sem.at[2]),
        pltpu.make_async_copy(combine_hbm, combine, small_sem.at[3]),
    ]
    for copy in first:
        copy.start()

    def gate_copy(k):
        part = pl.ds(pl.multiple_of(k * CHUNK, CHUNK), CHUNK)
        return pltpu.make_async_copy(gate_hbm.at[part, :], gate.at[k], gate_sem.at[k])

    def up_copy(k):
        part = pl.ds(pl.multiple_of(k * CHUNK, CHUNK), CHUNK)
        return pltpu.make_async_copy(up_hbm.at[part, :], up.at[k], up_sem.at[k])

    def down_copy(k):
        part = pl.ds(pl.multiple_of(k * CHUNK, CHUNK), CHUNK)
        return pltpu.make_async_copy(down_hbm.at[:, part], down.at[k], down_sem.at[k])

    last = chunks - 1
    tile = min(512, width)
    tiles = width // tile

    def late_copy(t, which):
        source, target = (gate_hbm, gate) if which == 0 else (up_hbm, up)
        lanes = slice(t * tile, (t + 1) * tile)
        return pltpu.make_async_copy(
            source.at[last * CHUNK:(last + 1) * CHUNK, lanes], target.at[last, :, lanes],
            late_sem.at[which, t],
        )

    def start_in(k, _):
        gate_copy(k).start()
        up_copy(k).start()
        return 0

    def start_down(k, _):
        down_copy(k).start()
        return 0

    start_in(0, 0)
    for peer in peers:
        pl.semaphore_signal(barrier, inc=1, device_id={"expert": peer})
    early = min(EARLY, last)
    lax.fori_loop(1, early, start_in, 0)

    outs = slice(0, 1), slice(1, chunks)
    mid = (chunks + 1) // 2
    backs = slice(0, mid), slice(mid, chunks)

    def block_of(k):
        return pl.ds(pl.multiple_of(k * MAIN, MAIN), MAIN)

    def send_main(k, peer, source):
        return pltpu.make_async_remote_copy(
            src_ref=send_m.at[k, peer], dst_ref=rows.at[k, block_of(source), :],
            send_sem=send_sem.at[k, peer], recv_sem=recv_sem.at[k, source], device_id={"expert": peer},
        )

    def send_extra(half, peer, source):
        return pltpu.make_async_remote_copy(
            src_ref=send_e.at[peer, outs[half]], dst_ref=recv_e.at[source, outs[half]],
            send_sem=send_e_sem.at[half, peer], recv_sem=recv_e_sem.at[half, source],
            device_id={"expert": peer},
        )

    def back_main(k, peer, source):
        return pltpu.make_async_remote_copy(
            src_ref=back_m.at[k, peer], dst_ref=home.at[k, block_of(source), :],
            send_sem=back_sem.at[k, peer], recv_sem=home_sem.at[k, source], device_id={"expert": peer},
        )

    def back_extra(half, peer, source):
        return pltpu.make_async_remote_copy(
            src_ref=back_e.at[peer, backs[half]], dst_ref=home_e.at[source, backs[half]],
            send_sem=back_e_sem.at[half, peer], recv_sem=home_e_sem.at[half, source],
            device_id={"expert": peer},
        )

    def to_all(copy, at):
        for peer in peers:
            copy(at, peer, me).start()

    def from_all(copy, at):
        for peer in peers:
            copy(at, peer, peer).wait_recv()

    def sent_all(copy, at):
        for peer in peers:
            copy(at, peer, me).wait_send()

    row = iota((height, count), 0)
    tail = row - mains
    block = jnp.where(row < mains, row // MAIN, jnp.where(tail < extras, tail // EXTRA, -1))
    slot = jnp.where(row < mains, row % MAIN, MAIN + tail % EXTRA)
    earlier = (iota((count, count), 0) < iota((count, count), 1)).astype(F32).astype(BF16)

    full = rows.shape[1]
    rows[:, height:, :] = jnp.zeros((chunks, full - height, CHUNK), BF16)
    hidden[height:, :] = jnp.zeros((full - height, width), BF16)

    first[0].wait()
    own = ids[...]
    member = iota((8, count), 0) == own
    ranks = dot(member.astype(F32).astype(BF16), earlier)
    place = jnp.sum(jnp.where(member, ranks, 0.0), axis=0, keepdims=True).astype(I32)
    low, high = own * span, own * span + span
    mask = (block >= low) & (block < high) & (slot == place)
    pick = jnp.where(mask, 1.0, 0.0).astype(BF16)

    def fold_extra(k, extra):
        for j in range(PIECES):
            fold[k, pl.ds(j, extras, stride=PIECES), :] = extra[:, j * LANES:(j + 1) * LANES]
        return fold[k, :n * FOLD].reshape(n, FOLD, LANES).astype(BF16)

    def push_main(k, block_m):
        send_m[k] = block_m.astype(BF16).reshape(n, MAIN, CHUNK)
        to_all(send_main, k)
        rows[k, block_of(me), :] = send_m[k, me]

    def push_extra(half):
        to_all(send_extra, half)
        recv_e[me, outs[half]] = send_e[me, outs[half]]

    first[1].wait()
    picked = dot(pick, tokens[:, lead])
    send_e[:, 0] = fold_extra(0, picked[mains:mains + extras])
    pl.semaphore_wait(barrier, n - 1)
    push_extra(0)
    push_main(0, picked[:mains])
    first[2].wait()
    picked = dot(pick[mains:], tokens[:, rest])
    for k in range(1, chunks):
        send_e[:, k] = fold_extra(k, picked[:extras, (k - 1) * CHUNK:k * CHUNK])
    push_extra(1)
    for k in range(1, chunks):
        push_main(k, dot(pick[:mains], tokens[:, k * CHUNK:(k + 1) * CHUNK]))

    first[3].wait()
    weight = combine[...].astype(F32)
    put = jnp.transpose(jnp.where(mask, weight, 0.0)).astype(BF16)

    def unfold(source, target, part):
        blank = jnp.zeros((height - mains - extras, CHUNK), F32)
        for k in range(part.start, part.stop):
            fold[k, :n * FOLD] = source[:, k].astype(F32).reshape(n * FOLD, LANES)
            parts = [fold[k, pl.ds(j, extras, stride=PIECES), :] for j in range(PIECES)]
            whole = jnp.concatenate(parts, axis=1)
            if height > mains + extras:
                whole = jnp.concatenate([whole, blank], axis=0)
            target[k, mains:height, :] = whole.astype(BF16)

    def arrive(k):
        gate_copy(k).wait()
        up_copy(k).wait()
        from_all(send_main, k)

    lax.fori_loop(early, last, start_in, 0)
    for t in range(tiles):
        for which in range(2):
            late_copy(t, which).start()

    from_all(send_extra, 0)
    unfold(recv_e, rows, outs[0])
    arrive(0)
    gate_sum[...] = dot(rows[0], gate[0])
    up_sum[...] = dot(rows[0], up[0])
    from_all(send_extra, 1)
    unfold(recv_e, rows, outs[1])

    def project(k, _):
        arrive(k)
        gate_sum[...] += dot(rows[k], gate[k])
        up_sum[...] += dot(rows[k], up[k])
        return 0

    for k in range(1, last):
        project(k, 0)
        if k == DOWN_AT:
            lax.fori_loop(0, DOWN_N, start_down, 0)
        if k == last - 1:
            lax.fori_loop(DOWN_N, chunks, start_down, 0)
    from_all(send_main, last)

    def activate(t):
        part = slice(t * tile, (t + 1) * tile)
        g = gate_sum[:height, part]
        hidden[:height, part] = (g / (1.0 + jnp.exp(-g)) * up_sum[:height, part]).astype(BF16)

    for t in range(tiles):
        part = slice(t * tile, (t + 1) * tile)
        late_copy(t, 0).wait()
        late_copy(t, 1).wait()
        gate_sum[:, part] += dot(rows[last], gate[last, :, part])
        up_sum[:, part] += dot(rows[last], up[last, :, part])
        if t > 0:
            activate(t - 1)
    activate(tiles - 1)

    def finish(k):
        down_copy(k).wait()
        result = dot(hidden[...], down[k])
        back_m[k] = result[:mains].astype(BF16).reshape(n, MAIN, CHUNK)
        return result[mains:mains + extras]

    def pack_extra(k, extra):
        back_e[:, k] = fold_extra(k, extra)

    def give_back(k):
        to_all(back_main, k)
        home[k, block_of(me), :] = back_m[k, me]

    def give_extra(half):
        to_all(back_extra, half)
        home_e[me, backs[half]] = back_e[me, backs[half]]

    def step(k, _):
        extra = finish(k)
        give_back(k)
        pack_extra(k, extra)
        return 0

    lax.fori_loop(0, mid, step, 0)
    give_extra(0)
    lax.fori_loop(mid, last, step, 0)
    pack_extra(last, finish(last))
    give_extra(1)
    give_back(last)

    def combine_chunk(k):
        from_all(back_main, k)
        part = pl.ds(pl.multiple_of(k * CHUNK, CHUNK), CHUNK)
        out_vmem[:, part] = dot(put, home[k]).astype(BF16)

    def collect(k, _):
        combine_chunk(k)
        sent_all(back_main, k)
        return 0

    def drain(k, _):
        sent_all(send_main, k)
        return 0

    lax.fori_loop(0, chunks, drain, 0)
    sent_all(send_extra, 0)
    sent_all(send_extra, 1)
    for half in range(2):
        from_all(back_extra, half)
        unfold(home_e, home, backs[half])
        sent_all(back_extra, half)
        lax.fori_loop(backs[half].start, min(backs[half].stop, last), collect, 0)
    combine_chunk(last)
    sent_all(back_main, last)


def local(tokens, expert_ids, combine, w_gate, w_up, w_down):
    n = lax.axis_size("expert")
    span = n // EXPERTS
    count, model_width = tokens.shape
    width = w_gate.shape[1]
    chunks = model_width // CHUNK
    height = n * MAIN + extra_height(n)
    dma = pltpu.SemaphoreType.DMA
    vmem = pltpu.VMEM
    anywhere = pl.BlockSpec(memory_space=pltpu.HBM)
    packed = (n, chunks, FOLD, LANES)
    return pl.pallas_call(
        functools.partial(kernel, n, span, chunks),
        out_shape=pltpu.VMEM((count, model_width), BF16),
        in_specs=[anywhere] * 6,
        out_specs=pl.BlockSpec(memory_space=pltpu.VMEM),
        scratch_shapes=[
            vmem((count, model_width), BF16),
            vmem((1, count), I32),
            vmem((1, count), BF16),
            vmem((chunks, CHUNK, width), BF16),
            vmem((chunks, CHUNK, width), BF16),
            vmem((chunks, width, CHUNK), BF16),
            vmem((chunks, n, MAIN, CHUNK), BF16),
            vmem(packed, BF16),
            vmem((chunks, padded(height), CHUNK), BF16),
            vmem(packed, BF16),
            vmem((chunks, (n + 1) * FOLD, LANES), F32),
            vmem((padded(height), width), F32),
            vmem((padded(height), width), F32),
            vmem((padded(height), width), BF16),
            vmem((chunks, n, MAIN, CHUNK), BF16),
            vmem(packed, BF16),
            vmem((chunks, height, CHUNK), BF16),
            vmem(packed, BF16),
            dma((4,)),
            dma((2, max(1, width // 512))),
            dma((chunks,)),
            dma((chunks,)),
            dma((chunks,)),
            dma((chunks, n)),
            dma((chunks, n)),
            dma((chunks, n)),
            dma((chunks, n)),
            dma((2, n)),
            dma((2, n)),
            dma((2, n)),
            dma((2, n)),
        ],
        compiler_params=pltpu.CompilerParams(
            collective_id=0, vmem_limit_bytes=54 * 1024 * 1024
        ),
    )(
        tokens,
        expert_ids.reshape(1, count),
        combine.reshape(1, count),
        w_gate,
        w_up,
        w_down,
    )


def solution(mesh):
    placed = (
        P(("dp", "expert"), None),
        P(("dp", "expert"), None),
        P(("dp", "expert"), None),
        P(None, "expert"),
        P(None, "expert"),
        P("expert", None),
    )
    return jax.shard_map(
        local, mesh=mesh, in_specs=placed, out_specs=P(("dp", "expert"), None), check_vma=False
    )
```

```python
import functools

import jax
import jax.numpy as jnp
from jax import lax
from jax.experimental import pallas as pl
from jax.experimental.pallas import tpu as pltpu
from jax.sharding import PartitionSpec as P

EXPERTS = 4
TOP = 1
CAP = 18
MAIN = 16
EXTRA = CAP - MAIN
FOLD = 8
LANES = 128
PIECES = FOLD // EXTRA
CHUNK = PIECES * LANES
SPAN_ROWS = 128
EARLY, DOWN_AT, DOWN_N = 6, 2, 2
BF16, F32, I32 = jnp.bfloat16, jnp.float32, jnp.int32


def iota(shape, axis):
    return lax.broadcasted_iota(I32, shape, axis)


def dot(a, b):
    return jnp.dot(a, b, preferred_element_type=F32)


def padded(height):
    return -(-height // SPAN_ROWS) * SPAN_ROWS


def extra_height(n):
    return -(-EXTRA * n // MAIN) * MAIN


def kernel(
    n, span, chunks, tokens_hbm, ids_hbm, combine_hbm, gate_hbm, up_hbm, down_hbm, out_vmem,
    tokens, ids, combine, gate, up, down, send_m, send_e, rows, recv_e, fold, gate_sum, up_sum,
    hidden, back_m, back_e, home, home_e,
    small_sem, late_sem, gate_sem, up_sem, down_sem, send_sem, recv_sem, back_sem, home_sem,
    send_e_sem, recv_e_sem, back_e_sem, home_e_sem,
):
    me = lax.axis_index("expert")
    count = tokens.shape[0]
    width = gate.shape[2]
    mains = n * MAIN
    extras = n * EXTRA
    height = mains + extra_height(n)
    chip, core = me // 2, me % 2

    peers = []
    for step in range(1, n // 2):
        for turn in range(2):
            peers.append((chip + step) % (n // 2) * 2 + (core + turn) % 2)
    peers.append(chip * 2 + (core + 1) % 2)

    barrier = pltpu.get_barrier_semaphore()
    lead, rest = slice(0, CHUNK), slice(CHUNK, chunks * CHUNK)
    first = [
        pltpu.make_async_copy(ids_hbm, ids, small_sem.at[0]),
        pltpu.make_async_copy(tokens_hbm.at[:, lead], tokens.at[:, lead], small_sem.at[1]),
        pltpu.make_async_copy(tokens_hbm.at[:, rest], tokens.at[:, rest], small_sem.at[2]),
        pltpu.make_async_copy(combine_hbm, combine, small_sem.at[3]),
    ]
    for copy in first:
        copy.start()

    def gate_copy(k):
        part = pl.ds(pl.multiple_of(k * CHUNK, CHUNK), CHUNK)
        return pltpu.make_async_copy(gate_hbm.at[part, :], gate.at[k], gate_sem.at[k])

    def up_copy(k):
        part = pl.ds(pl.multiple_of(k * CHUNK, CHUNK), CHUNK)
        return pltpu.make_async_copy(up_hbm.at[part, :], up.at[k], up_sem.at[k])

    def down_copy(k):
        part = pl.ds(pl.multiple_of(k * CHUNK, CHUNK), CHUNK)
        return pltpu.make_async_copy(down_hbm.at[:, part], down.at[k], down_sem.at[k])

    last = chunks - 1
    tile = min(512, width)
    tiles = width // tile

    def late_copy(t, which):
        source, target = (gate_hbm, gate) if which == 0 else (up_hbm, up)
        lanes = slice(t * tile, (t + 1) * tile)
        return pltpu.make_async_copy(
            source.at[last * CHUNK:(last + 1) * CHUNK, lanes], target.at[last, :, lanes],
            late_sem.at[which, t],
        )

    def start_in(k, _):
        gate_copy(k).start()
        up_copy(k).start()
        return 0

    def start_down(k, _):
        down_copy(k).start()
        return 0

    start_in(0, 0)
    for peer in peers:
        pl.semaphore_signal(barrier, inc=1, device_id={"expert": peer})
    early = min(EARLY, last)
    lax.fori_loop(1, early, start_in, 0)

    outs = slice(0, 1), slice(1, chunks)
    mid = (chunks + 1) // 2
    backs = slice(0, mid), slice(mid, chunks)

    def block_of(k):
        return pl.ds(pl.multiple_of(k * MAIN, MAIN), MAIN)

    def send_main(k, peer, source):
        return pltpu.make_async_remote_copy(
            src_ref=send_m.at[k, peer], dst_ref=rows.at[k, block_of(source), :],
            send_sem=send_sem.at[k, peer], recv_sem=recv_sem.at[k, source], device_id={"expert": peer},
        )

    def send_extra(half, peer, source):
        return pltpu.make_async_remote_copy(
            src_ref=send_e.at[peer, outs[half]], dst_ref=recv_e.at[source, outs[half]],
            send_sem=send_e_sem.at[half, peer], recv_sem=recv_e_sem.at[half, source],
            device_id={"expert": peer},
        )

    def back_main(k, peer, source):
        return pltpu.make_async_remote_copy(
            src_ref=back_m.at[k, peer], dst_ref=home.at[k, block_of(source), :],
            send_sem=back_sem.at[k, peer], recv_sem=home_sem.at[k, source], device_id={"expert": peer},
        )

    def back_extra(half, peer, source):
        return pltpu.make_async_remote_copy(
            src_ref=back_e.at[peer, backs[half]], dst_ref=home_e.at[source, backs[half]],
            send_sem=back_e_sem.at[half, peer], recv_sem=home_e_sem.at[half, source],
            device_id={"expert": peer},
        )

    def to_all(copy, at):
        for peer in peers:
            copy(at, peer, me).start()

    def from_all(copy, at):
        for peer in peers:
            copy(at, peer, peer).wait_recv()

    def sent_all(copy, at):
        for peer in peers:
            copy(at, peer, me).wait_send()

    row = iota((height, count), 0)
    tail = row - mains
    block = jnp.where(row < mains, row // MAIN, jnp.where(tail < extras, tail // EXTRA, -1))
    slot = jnp.where(row < mains, row % MAIN, MAIN + tail % EXTRA)
    earlier = (iota((count, count), 0) < iota((count, count), 1)).astype(F32).astype(BF16)

    full = rows.shape[1]
    rows[:, height:, :] = jnp.zeros((chunks, full - height, CHUNK), BF16)
    hidden[height:, :] = jnp.zeros((full - height, width), BF16)

    first[0].wait()
    own = ids[...]
    member = iota((8, count), 0) == own
    ranks = dot(member.astype(F32).astype(BF16), earlier)
    place = jnp.sum(jnp.where(member, ranks, 0.0), axis=0, keepdims=True).astype(I32)
    low, high = own * span, own * span + span
    mask = (block >= low) & (block < high) & (slot == place)
    pick = jnp.where(mask, 1.0, 0.0).astype(BF16)

    def fold_extra(k, extra):
        for j in range(PIECES):
            fold[k, pl.ds(j, extras, stride=PIECES), :] = extra[:, j * LANES:(j + 1) * LANES]
        return fold[k, :n * FOLD].reshape(n, FOLD, LANES).astype(BF16)

    def push_main(k, block_m):
        send_m[k] = block_m.astype(BF16).reshape(n, MAIN, CHUNK)
        to_all(send_main, k)
        rows[k, block_of(me), :] = send_m[k, me]

    def push_extra(half):
        to_all(send_extra, half)
        recv_e[me, outs[half]] = send_e[me, outs[half]]

    first[1].wait()
    picked = dot(pick, tokens[:, lead])
    send_e[:, 0] = fold_extra(0, picked[mains:mains + extras])
    pl.semaphore_wait(barrier, n - 1)
    push_extra(0)
    push_main(0, picked[:mains])
    first[2].wait()
    picked = dot(pick[mains:], tokens[:, rest])
    for k in range(1, chunks):
        send_e[:, k] = fold_extra(k, picked[:extras, (k - 1) * CHUNK:k * CHUNK])
    push_extra(1)
    for k in range(1, chunks):
        push_main(k, dot(pick[:mains], tokens[:, k * CHUNK:(k + 1) * CHUNK]))

    first[3].wait()
    weight = combine[...].astype(F32)
    put = jnp.transpose(jnp.where(mask, weight, 0.0)).astype(BF16)

    def unfold(source, target, part):
        blank = jnp.zeros((height - mains - extras, CHUNK), F32)
        for k in range(part.start, part.stop):
            fold[k, :n * FOLD] = source[:, k].astype(F32).reshape(n * FOLD, LANES)
            parts = [fold[k, pl.ds(j, extras, stride=PIECES), :] for j in range(PIECES)]
            whole = jnp.concatenate(parts, axis=1)
            if height > mains + extras:
                whole = jnp.concatenate([whole, blank], axis=0)
            target[k, mains:height, :] = whole.astype(BF16)

    def arrive(k):
        gate_copy(k).wait()
        up_copy(k).wait()
        from_all(send_main, k)

    lax.fori_loop(early, last, start_in, 0)
    for t in range(tiles):
        for which in range(2):
            late_copy(t, which).start()

    from_all(send_extra, 0)
    unfold(recv_e, rows, outs[0])
    arrive(0)
    gate_sum[...] = dot(rows[0], gate[0])
    up_sum[...] = dot(rows[0], up[0])
    from_all(send_extra, 1)
    unfold(recv_e, rows, outs[1])

    def project(k, _):
        arrive(k)
        gate_sum[...] += dot(rows[k], gate[k])
        up_sum[...] += dot(rows[k], up[k])
        return 0

    for k in range(1, last):
        project(k, 0)
        if k == DOWN_AT:
            lax.fori_loop(0, DOWN_N, start_down, 0)
        if k == last - 1:
            lax.fori_loop(DOWN_N, chunks, start_down, 0)
    from_all(send_main, last)

    def activate(t):
        part = slice(t * tile, (t + 1) * tile)
        g = gate_sum[:height, part]
        hidden[:height, part] = (g / (1.0 + jnp.exp(-g)) * up_sum[:height, part]).astype(BF16)

    for t in range(tiles):
        part = slice(t * tile, (t + 1) * tile)
        late_copy(t, 0).wait()
        late_copy(t, 1).wait()
        gate_sum[:, part] += dot(rows[last], gate[last, :, part])
        up_sum[:, part] += dot(rows[last], up[last, :, part])
        if t > 0:
            activate(t - 1)
    activate(tiles - 1)

    def finish(k):
        down_copy(k).wait()
        result = dot(hidden[...], down[k])
        back_m[k] = result[:mains].astype(BF16).reshape(n, MAIN, CHUNK)
        return result[mains:mains + extras]

    def pack_extra(k, extra):
        back_e[:, k] = fold_extra(k, extra)

    def give_back(k):
        to_all(back_main, k)
        home[k, block_of(me), :] = back_m[k, me]

    def give_extra(half):
        to_all(back_extra, half)
        home_e[me, backs[half]] = back_e[me, backs[half]]

    def step(k, _):
        extra = finish(k)
        give_back(k)
        pack_extra(k, extra)
        return 0

    for k in range(mid):
        step(k, 0)
    give_extra(0)
    for k in range(mid, last):
        step(k, 0)
    pack_extra(last, finish(last))
    give_extra(1)
    give_back(last)

    def combine_chunk(k):
        from_all(back_main, k)
        part = pl.ds(pl.multiple_of(k * CHUNK, CHUNK), CHUNK)
        out_vmem[:, part] = dot(put, home[k]).astype(BF16)

    def collect(k, _):
        combine_chunk(k)
        sent_all(back_main, k)
        return 0

    def drain(k, _):
        sent_all(send_main, k)
        return 0

    lax.fori_loop(0, chunks, drain, 0)
    sent_all(send_extra, 0)
    sent_all(send_extra, 1)
    for half in range(2):
        from_all(back_extra, half)
        unfold(home_e, home, backs[half])
        sent_all(back_extra, half)
        lax.fori_loop(backs[half].start, min(backs[half].stop, last), collect, 0)
    combine_chunk(last)
    sent_all(back_main, last)


def local(tokens, expert_ids, combine, w_gate, w_up, w_down):
    n = lax.axis_size("expert")
    span = n // EXPERTS
    count, model_width = tokens.shape
    width = w_gate.shape[1]
    chunks = model_width // CHUNK
    height = n * MAIN + extra_height(n)
    dma = pltpu.SemaphoreType.DMA
    vmem = pltpu.VMEM
    anywhere = pl.BlockSpec(memory_space=pltpu.HBM)
    packed = (n, chunks, FOLD, LANES)
    return pl.pallas_call(
        functools.partial(kernel, n, span, chunks),
        out_shape=pltpu.VMEM((count, model_width), BF16),
        in_specs=[anywhere] * 6,
        out_specs=pl.BlockSpec(memory_space=pltpu.VMEM),
        scratch_shapes=[
            vmem((count, model_width), BF16),
            vmem((1, count), I32),
            vmem((1, count), BF16),
            vmem((chunks, CHUNK, width), BF16),
            vmem((chunks, CHUNK, width), BF16),
            vmem((chunks, width, CHUNK), BF16),
            vmem((chunks, n, MAIN, CHUNK), BF16),
            vmem(packed, BF16),
            vmem((chunks, padded(height), CHUNK), BF16),
            vmem(packed, BF16),
            vmem((chunks, (n + 1) * FOLD, LANES), F32),
            vmem((padded(height), width), F32),
            vmem((padded(height), width), F32),
            vmem((padded(height), width), BF16),
            vmem((chunks, n, MAIN, CHUNK), BF16),
            vmem(packed, BF16),
            vmem((chunks, height, CHUNK), BF16),
            vmem(packed, BF16),
            dma((4,)),
            dma((2, max(1, width // 512))),
            dma((chunks,)),
            dma((chunks,)),
            dma((chunks,)),
            dma((chunks, n)),
            dma((chunks, n)),
            dma((chunks, n)),
            dma((chunks, n)),
            dma((2, n)),
            dma((2, n)),
            dma((2, n)),
            dma((2, n)),
        ],
        compiler_params=pltpu.CompilerParams(
            collective_id=0, vmem_limit_bytes=54 * 1024 * 1024
        ),
    )(
        tokens,
        expert_ids.reshape(1, count),
        combine.reshape(1, count),
        w_gate,
        w_up,
        w_down,
    )


def solution(mesh):
    placed = (
        P(("dp", "expert"), None),
        P(("dp", "expert"), None),
        P(("dp", "expert"), None),
        P(None, "expert"),
        P(None, "expert"),
        P("expert", None),
    )
    return jax.shard_map(
        local, mesh=mesh, in_specs=placed, out_specs=P(("dp", "expert"), None), check_vma=False
    )
```
